32 devices in a mesh: pipe: 4 (over y, core), expert: 2 (over x), dp: 4 (over z).
Axes of the slice: x: 2, y: 2, z: 4, core: 2. Of those that a mesh axis runs over, the one named last changes fastest.
Arguments:
- tokens: bfloat16 [4, 1024, 3072], P('pipe', ('expert', 'dp')), may hold values from -6 to 6
- grad_out: bfloat16 [4, 1024, 3072], P('pipe', ('expert', 'dp')), may hold values from -6 to 6
- routes: int32 [4, 1024, 2], P('pipe', ('expert', 'dp')), may hold values from 0 to 7, as said below
- route_weights: float32 [4, 1024, 2], P('pipe', ('expert', 'dp')), may hold values from 0.1 to 0.9
- gate_weight: bfloat16 [4, 3072, 32768], P('pipe', None, ('expert', 'dp')), may hold values from -0.109375 to 0.109375
- up_weight: bfloat16 [4, 3072, 32768], P('pipe', None, ('expert', 'dp')), may hold values from -0.109375 to 0.109375
- down_weight: bfloat16 [4, 32768, 3072], P('pipe', ('expert', 'dp')), may hold values from -0.046875 to 0.046875
Outputs:
- upstream: bfloat16 [4, 1024, 3072], P('pipe', ('expert', 'dp'))
The draws below stay inside these ranges and needn't reach their ends.
Inputs may be any that keep to these rules, and one draw needn't show every extreme that they name: `routes`: each row names two different experts. In every section, for each window expert e < 2, the tokens of one device that name e number 1 to 8, exactly 8 on some device, and the tokens of the whole section name e exactly 36 times.
All inputs are finite; a program needn't handle non-finite values.
Results may differ from the reference program's by a relative error of at most 0.0013.
Values may be sent and summed in bfloat16 or wider, within the bound.
No kernel may reach another device: no remote copies, remote signals or barrier semaphores. Data moves between devices by JAX's collectives and lax.ppermute only.
A program may use at most 192 MiB of HBM per device.

```python
import jax
import jax.numpy as jnp
from jax import lax

D = 3072
FF = 16384
EXPERTS = 8
EF = 2
CAP = 8
TOK_DEV = 128
SECTIONS = 4
TOKENS = 1024
HID_DEV = 4096
PACKED = 36


def draw_routes(key, part):
    blocks = TOKENS // TOK_DEV
    half_blocks = blocks // 2

    def section_draw(section_key):
        chosen_sets = []
        for expert in range(2):
            expert_key = jax.random.fold_in(section_key, expert)
            key_counts, key_forced, key_shuffle, key_scores = jax.random.split(expert_key, 4)
            drawn = jax.random.randint(key_counts, (half_blocks,), 1, CAP + 1)
            forced = jax.random.randint(key_forced, (), 0, half_blocks)
            drawn = jnp.where(jnp.arange(half_blocks) == forced, CAP, drawn)
            paired = jnp.concatenate([drawn, CAP + 1 - drawn])
            shuffle = jax.random.permutation(key_shuffle, blocks)
            counts = paired[shuffle]
            scores = jax.random.randint(key_scores, (blocks, TOK_DEV), 0, 1048576) * TOK_DEV + jnp.arange(TOK_DEV)[None, :]
            rank_of = jnp.argsort(jnp.argsort(scores, axis=1, stable=True), axis=1, stable=True)
            chosen_sets.append((rank_of < counts[:, None]).reshape(-1))
        other_key = jax.random.fold_in(section_key, 7)
        key_first, key_step = jax.random.split(other_key, 2)
        other_first = jax.random.randint(key_first, (TOKENS,), 2, EXPERTS)
        other_step = jax.random.randint(key_step, (TOKENS,), 1, EXPERTS - 2)
        other_second = 2 + (other_first - 2 + other_step) % (EXPERTS - 2)
        chosen_zero = chosen_sets[0]
        chosen_one = chosen_sets[1]
        first_pick = jnp.where(chosen_zero, 0, jnp.where(chosen_one, 1, other_first))
        second_pick = jnp.where(chosen_zero & chosen_one, 1, jnp.where(chosen_zero | chosen_one, other_first, other_second))
        return jnp.stack([first_pick, second_pick], axis=-1).astype(jnp.int32)
    section_keys = jax.random.split(key, SECTIONS)
    return jax.vmap(section_draw)(section_keys)


def shard_levels(own_key, shape, cuts, low, high):
    loudness, own = 1.0, jax.random.fold_in(own_key, 6)
    for position, parts in cuts:
        heights = jnp.exp(jax.random.uniform(jax.random.fold_in(own, position), (parts,), jnp.float32, low / len(cuts), high / len(cuts)))
        loudness = loudness * jnp.repeat(heights, shape[position] // parts).reshape([-1 if axis == position else 1 for axis in range(len(shape))])
    return loudness


def gaussian(rng, dims, deviation, bound, shards=(), kind=jnp.bfloat16):
    entries = deviation * jax.random.normal(rng, dims, jnp.float32)
    if shards:
        entries = entries * shard_levels(rng, dims, shards, -0.22, 0.18)
    return jnp.clip(entries, -bound, bound).astype(kind)


def setup_inputs(seed: int = 0) -> dict:
    arg_keys = jax.random.split(jax.random.key(seed), 8)
    return {
        "tokens": gaussian(arg_keys[0], (SECTIONS, TOKENS, D), 1.0, 6.0, ((0, 4), (1, 8))),
        "grad_out": gaussian(arg_keys[1], (SECTIONS, TOKENS, D), 1.0, 6.0, ((0, 4), (1, 8))),
        "routes": draw_routes(jax.random.fold_in(arg_keys[7], 71), 0),
        "route_weights": jnp.clip(0.1 + 0.79999997 * jax.random.uniform(arg_keys[3], (SECTIONS, TOKENS, 2), jnp.float32) ** shard_levels(arg_keys[3], (SECTIONS, TOKENS, 2), ((0, 4), (1, 8)), -0.2, 0.2), 0.1, 0.9),
        "gate_weight": gaussian(arg_keys[4], (SECTIONS, D, EF * FF), D ** -0.5, 0.109375, ((0, 4), (2, 8))),
        "up_weight": gaussian(arg_keys[5], (SECTIONS, D, EF * FF), D ** -0.5, 0.109375, ((0, 4), (2, 8))),
        "down_weight": gaussian(arg_keys[6], (SECTIONS, EF * FF, D), FF ** -0.5, 0.046875, ((0, 4), (1, 8))),
    }


def hidden_parts(rows_in, rows_grad, gate_cols, up_cols, down_rows, shard_width):
    gate_pre = jnp.dot(rows_in, gate_cols, preferred_element_type=jnp.float32)
    up_pre = jnp.dot(rows_in, up_cols, preferred_element_type=jnp.float32)
    sigmoid_gate = jax.nn.sigmoid(gate_pre)
    contract = (((1,), (1,)), ((), ()))
    act_grad = lax.dot_general(rows_grad, down_rows, contract, preferred_element_type=jnp.float32)
    gate_grad = (act_grad * up_pre * sigmoid_gate * (1.0 + gate_pre * (1.0 - sigmoid_gate))).astype(jnp.bfloat16)
    up_grad = (act_grad * gate_pre * sigmoid_gate).astype(jnp.bfloat16)
    shard_total = gate_cols.shape[1] // shard_width

    def one_shard(shard_index):
        start = shard_index * shard_width
        gate_piece = lax.dynamic_slice_in_dim(gate_grad, start, shard_width, 1)
        up_piece = lax.dynamic_slice_in_dim(up_grad, start, shard_width, 1)
        gate_block = lax.dynamic_slice_in_dim(gate_cols, start, shard_width, 1)
        up_block = lax.dynamic_slice_in_dim(up_cols, start, shard_width, 1)
        value = lax.dot_general(gate_piece, gate_block, contract, preferred_element_type=jnp.float32)
        value = value + lax.dot_general(up_piece, up_block, contract, preferred_element_type=jnp.float32)
        return value.astype(jnp.bfloat16)

    shard_parts = lax.map(one_shard, jnp.arange(shard_total, dtype=jnp.int32))
    return jnp.sum(shard_parts.astype(jnp.float32), axis=0)


def reference(tokens, grad_out, routes, route_weights, gate_weight, up_weight, down_weight):
    results = []
    for section_index in range(SECTIONS):
        inputs = tokens[section_index]
        upstream_grad = grad_out[section_index].astype(jnp.float32)
        picks = routes[section_index]
        pick_weights = route_weights[section_index]
        branch = jnp.zeros((TOKENS, D), jnp.float32)
        for expert in range(EF):
            first_pick = picks[:, 0] == expert
            second_pick = picks[:, 1] == expert
            chosen = first_pick | second_pick
            weight = jnp.where(first_pick, pick_weights[:, 0], 0.0) + jnp.where(second_pick, pick_weights[:, 1], 0.0)
            scaled = (weight[:, None] * upstream_grad).astype(jnp.bfloat16)
            row_index = jnp.nonzero(chosen, size=PACKED)[0].astype(jnp.int32)
            gate_cols = gate_weight[section_index][:, expert * FF:(expert + 1) * FF]
            up_cols = up_weight[section_index][:, expert * FF:(expert + 1) * FF]
            down_rows = down_weight[section_index][expert * FF:(expert + 1) * FF, :]
            expert_grad = hidden_parts(inputs[row_index], scaled[row_index], gate_cols, up_cols, down_rows, HID_DEV)
            branch = branch.at[row_index].add(expert_grad)
        results.append((upstream_grad + branch).astype(jnp.bfloat16))
    grads = jnp.stack(results)
    return jnp.concatenate([grads[1:], jnp.zeros_like(grads[:1])], axis=0)
```

```python
import functools

import jax
import jax.numpy as jnp
from jax import lax
from jax.experimental import pallas as pl
from jax.experimental.pallas import tpu as pltpu
from jax.sharding import PartitionSpec as P

EF = 2
CAP = 8
MIB = 1 << 20
F32 = jnp.float32
BF16 = jnp.bfloat16
NN = (((1,), (0,)), ((), ()))
NT = (((1,), (1,)), ((), ()))
TN = (((0,), (0,)), ((), ()))
VMEM = pl.BlockSpec(memory_space=pltpu.VMEM)
ANY = pl.BlockSpec(memory_space=pl.ANY)


def dot(a, b, dims):
    return lax.dot_general(a, b, dims, preferred_element_type=F32)


def slot_table(picks, expert):
    count = picks.shape[0]
    chosen = jnp.any(picks == expert, axis=1, keepdims=True)
    rows = lax.broadcasted_iota(jnp.int32, (count, count), 0)
    columns = lax.broadcasted_iota(jnp.int32, (count, count), 1)
    before = (columns < rows).astype(BF16)
    flags = jnp.broadcast_to(chosen, (count, 128)).astype(F32).astype(BF16)
    place = dot(before, flags, NN)[:, :CAP]
    slots = lax.broadcasted_iota(jnp.int32, (count, CAP), 1).astype(F32)
    return jnp.where((place == slots) & chosen, 1.0, 0.0)


def route_body(tokens, grad_out, picks_ref, weights_ref, rows_in, rows_grad):
    picks = picks_ref[...]
    pick_weights = weights_ref[...]
    group = rows_in.shape[0] // EF
    upstream = grad_out[...].astype(F32)
    for expert in range(EF):
        table = slot_table(picks, expert).astype(BF16)
        weight = jnp.sum(jnp.where(picks == expert, pick_weights, 0.0), axis=1, keepdims=True)
        scaled = (weight * upstream).astype(BF16)
        sent_in = dot(table, tokens[...], TN).astype(BF16)
        sent_grad = dot(table, scaled, TN).astype(BF16)
        for member in range(group):
            rows_in[expert * group + member] = sent_in
            rows_grad[expert * group + member] = sent_grad


def act_body(rows_grad, down, act_grad, buffers, sems, *, block):
    hidden = down.shape[0]
    count = hidden // block
    depth = buffers.shape[0]

    def fetch(index):
        slot = index % depth
        return pltpu.make_async_copy(down.at[pl.ds(index * block, block), :], buffers.at[slot], sems.at[slot])

    for index in range(min(depth, count)):
        fetch(index).start()
    for index in range(count):
        fetch(index).wait()
        value = dot(buffers[index % depth], rows_grad[...], NT)
        if index + depth < count:
            fetch(index + depth).start()
        act_grad[:, pl.ds(index * block, block)] = value.T


def back_body(rows_in, act_grad, gate, up, out, total, gates, ups, sems, *, block, chunk):
    slots = act_grad.shape[0]
    width, hidden = gate.shape
    count = hidden // block
    depth = gates.shape[0]

    def fetch(index):
        slot = index % depth
        part = pl.ds(index * block, block)
        return (
            pltpu.make_async_copy(gate.at[:, part], gates.at[slot], sems.at[0, slot]),
            pltpu.make_async_copy(up.at[:, part], ups.at[slot], sems.at[1, slot]),
        )

    for index in range(min(depth, count)):
        for copy in fetch(index):
            copy.start()
    for index in range(count):
        part = pl.ds(index * block, block)
        slot = index % depth
        copies = fetch(index)
        copies[0].wait()
        gate_pre = dot(rows_in[...], gates[slot], NN)[:slots]
        copies[1].wait()
        up_pre = dot(rows_in[...], ups[slot], NN)[:slots]
        sigmoid = jax.nn.sigmoid(gate_pre)
        grad = act_grad[:, part]
        gate_grad = (grad * up_pre * sigmoid * (1.0 + gate_pre * (1.0 - sigmoid))).astype(BF16)
        up_grad = (grad * gate_pre * sigmoid).astype(BF16)
        for start in range(0, width, chunk):
            rows = pl.ds(start, chunk)
            value = dot(gates[slot, rows, :], gate_grad, NT) + dot(ups[slot, rows, :], up_grad, NT)
            if index > 0:
                value = value + total[rows, :]
            if index < count - 1:
                total[rows, :] = value
            else:
                out[:, rows] = value.T.astype(BF16)
        if index + depth < count:
            for copy in fetch(index + depth):
                copy.start()


def total_body(parts, total):
    group = parts.shape[0] // EF
    for expert in range(EF):
        value = parts[expert * group].astype(F32)
        for member in range(1, group):
            value = value + parts[expert * group + member].astype(F32)
        total[pl.ds(expert * CAP, CAP), :] = value


def place_body(base, picks_ref, total, out):
    picks = picks_ref[...]
    table = jnp.concatenate([slot_table(picks, expert) for expert in range(EF)], axis=1)
    branch = lax.dot_general(table, total[...], NN, precision=lax.Precision.HIGHEST, preferred_element_type=F32)
    out[...] = (base[...].astype(F32) + branch).astype(BF16)


def call(body, out_shape, args, in_specs, name, limit, **kwargs):
    single = not isinstance(out_shape, (list, tuple))
    return pl.pallas_call(
        body,
        out_shape=out_shape,
        in_specs=in_specs,
        out_specs=VMEM if single else [VMEM] * len(out_shape),
        name=name,
        compiler_params=pltpu.CompilerParams(vmem_limit_bytes=limit),
        **kwargs,
    )(*args)


def to_previous(value, axis="pipe"):
    count = lax.axis_size(axis)
    return lax.ppermute(value, axis, [(source, source - 1) for source in range(1, count)])


def exchange(value):
    return lax.all_to_all(value, ("expert", "dp"), split_axis=0, concat_axis=0, tiled=True)


def shards(tokens, grad_out, routes, route_weights, gate_weight, up_weight, down_weight):
    members = lax.axis_size("expert") * lax.axis_size("dp")
    inputs, upstream, picks, pick_weights = tokens[0], grad_out[0], routes[0], route_weights[0]
    count, width = inputs.shape
    gate, up, down = gate_weight[0], up_weight[0], down_weight[0]
    hidden = gate.shape[1]
    slots = members * CAP
    shape = jax.ShapeDtypeStruct

    bound = shape((members, CAP, width), BF16)
    sent_in, sent_grad = call(
        route_body, [bound, bound], (inputs, upstream, picks, pick_weights), [VMEM] * 4, "route", 32 * MIB
    )
    rows_grad = exchange(sent_grad).reshape(slots, width)
    rows_in = exchange(sent_in).reshape(slots, width)
    next_upstream = to_previous(upstream)
    next_picks = to_previous(picks)

    rows_in = jnp.pad(rows_in, ((0, max(0, 128 - slots)), (0, 0)))
    block = min(hidden, 512)
    depth = 4
    act_grad = call(
        functools.partial(act_body, block=block),
        shape((slots, hidden), F32),
        (rows_grad, down),
        [VMEM, ANY],
        "act",
        40 * MIB,
        scratch_shapes=[pltpu.VMEM((depth, block, width), BF16), pltpu.SemaphoreType.DMA((depth,))],
    )
    depth = 3
    partial = call(
        functools.partial(back_body, block=block, chunk=512),
        shape((slots, width), BF16),
        (rows_in, act_grad, gate, up),
        [VMEM, VMEM, ANY, ANY],
        "back",
        40 * MIB,
        scratch_shapes=[
            pltpu.VMEM((width, slots), F32),
            pltpu.VMEM((depth, width, block), BF16),
            pltpu.VMEM((depth, width, block), BF16),
            pltpu.SemaphoreType.DMA((2, depth)),
        ],
    )
    returned = exchange(partial.reshape(members, CAP, width))
    total = call(total_body, shape((EF * CAP, width), F32), (returned,), [VMEM], "total", 16 * MIB)
    next_total = to_previous(total)
    out = call(
        place_body, shape((count, width), BF16), (next_upstream, next_picks, next_total), [VMEM] * 3, "place", 16 * MIB
    )
    return out[None]


def solution(mesh):
    row = P("pipe", ("expert", "dp"), None)
    column = P("pipe", None, ("expert", "dp"))
    return jax.shard_map(
        shards,
        mesh=mesh,
        in_specs=(row, row, row, row, column, column, row),
        out_specs=row,
        check_vma=False,
    )
```

```python
import functools

import jax
import jax.numpy as jnp
from jax import lax
from jax.experimental import pallas as pl
from jax.experimental.pallas import tpu as pltpu
from jax.sharding import PartitionSpec as P

EF = 2
CAP = 8
MIB = 1 << 20
F32 = jnp.float32
BF16 = jnp.bfloat16
NN = (((1,), (0,)), ((), ()))
NT = (((1,), (1,)), ((), ()))
TN = (((0,), (0,)), ((), ()))
VMEM = pl.BlockSpec(memory_space=pltpu.VMEM)
SMEM = pl.BlockSpec(memory_space=pltpu.SMEM)
HBM = pl.BlockSpec(memory_space=pltpu.HBM)
AXES = ("pipe", "expert", "dp")


def dot(a, b, dims):
    return lax.dot_general(a, b, dims, preferred_element_type=F32)


def slot_table(picks, expert):
    count = picks.shape[1]
    chosen = (picks[0:1, :] == expert) | (picks[1:2, :] == expert)
    rows = lax.broadcasted_iota(jnp.int32, (count, count), 0)
    columns = lax.broadcasted_iota(jnp.int32, (count, count), 1)
    before = jnp.where(rows < columns, 1.0, 0.0).astype(BF16)
    flags = jnp.broadcast_to(jnp.where(chosen, 1.0, 0.0), (CAP, count))
    place = dot(flags.astype(BF16), before, NN)
    slots = lax.broadcasted_iota(jnp.int32, (CAP, count), 0).astype(F32)
    return jnp.where(place == slots, flags, 0.0)


def pick_weight(picks, pick_weights, expert):
    first = jnp.where(picks[0:1, :] == expert, pick_weights[0:1, :], 0.0)
    return first + jnp.where(picks[1:2, :] == expert, pick_weights[1:2, :], 0.0)


def select(experts, picks, pick_weights, tokens, upstream):
    tables = [slot_table(picks, expert) for expert in experts]
    weights = [
        jnp.sum(table * pick_weight(picks, pick_weights, expert), axis=1, keepdims=True)
        for table, expert in zip(tables, experts)
    ]
    table = jnp.concatenate(tables, axis=0).astype(BF16)
    sent_in = dot(table, tokens, NN).astype(BF16)
    sent_grad = (jnp.concatenate(weights, axis=0) * dot(table, upstream, NN)).astype(BF16)
    return sent_in, sent_grad


def load(sources, targets, sems):
    copies = [
        pltpu.make_async_copy(source, target, sems.at[index])
        for index, (source, target) in enumerate(zip(sources, targets))
    ]
    for copy in copies:
        copy.start()
    for copy in copies:
        copy.wait()
    return [target[...] for target in targets]


def route_body(own, picks, pick_weights, tokens, grad_out, kept_in, kept_grad, sent, *scratch):
    loaded = load((picks, pick_weights, tokens, grad_out), scratch[:-1], scratch[-1])
    first = own[0]
    rows_in, rows_grad = select((first, 1 - first), *loaded)
    kept_in[...] = rows_in[:CAP]
    kept_grad[...] = rows_grad[:CAP]
    sent[0] = rows_grad[CAP:]
    sent[1] = rows_in[CAP:]


def route_all_body(picks, pick_weights, tokens, grad_out, rows_in, rows_grad, *scratch):
    loaded = load((picks, pick_weights, tokens, grad_out), scratch[:-1], scratch[-1])
    sent_in, sent_grad = select(range(EF), *loaded)
    group = rows_in.shape[0] // EF
    for expert in range(EF):
        for member in range(group):
            rows_in[expert * group + member] = sent_in[expert * CAP : (expert + 1) * CAP]
            rows_grad[expert * group + member] = sent_grad[expert * CAP : (expert + 1) * CAP]


def join_body(kept_in, kept_grad, received, rows_in, rows_grad):
    rows_in[...] = jnp.concatenate([kept_in[...], received[1]], axis=0)
    rows_grad[...] = jnp.concatenate([kept_grad[...], received[0]], axis=0)


def act_body(*refs, pieces, block):
    down, act_grad, rows, buffers, sems = refs[pieces:]
    hidden = down.shape[0]
    count = hidden // block
    depth = buffers.shape[0]

    def fetch(index):
        slot = index % depth
        return pltpu.make_async_copy(down.at[pl.ds(index * block, block), :], buffers.at[slot], sems.at[slot])

    for index in range(min(depth, count)):
        fetch(index).start()
    gather(refs[:pieces], rows)
    for index in range(count):
        fetch(index).wait()
        act_grad[:, pl.ds(index * block, block)] = dot(rows[...], buffers[index % depth], NT)
        if index + depth < count:
            fetch(index + depth).start()


def gather(pieces, rows):
    start = 0
    for piece in pieces:
        size = piece.shape[0]
        rows[pl.ds(start, size), :] = piece[...]
        start += size
    if start < rows.shape[0]:
        rows[pl.ds(start, rows.shape[0] - start), :] = jnp.zeros((rows.shape[0] - start, rows.shape[1]), BF16)


def back_body(*refs, pieces, block, chunk, kept):
    act_grad, gate, up = refs[pieces : pieces + 3]
    outs = refs[pieces + 3 : 2 * pieces + 3]
    rows_in, total, *buffers, sems = refs[2 * pieces + 3 :]
    slots = act_grad.shape[0]
    size = slots // pieces
    width, hidden = gate.shape
    count = hidden // block
    depth = buffers[0].shape[0]
    sources = ((up,) if kept else (up, gate))

    def fetch(index):
        slot = index % depth
        part = pl.ds(index * block, block)
        return [
            pltpu.make_async_copy(source.at[:, part], buffer.at[slot], sems.at[order, slot])
            for order, (source, buffer) in enumerate(zip(sources, buffers))
        ]

    for index in range(min(depth, count)):
        for copy in reversed(fetch(index)):
            copy.start()
    gather(refs[:pieces], rows_in)
    for index in range(count):
        part = pl.ds(index * block, block)
        slot = index % depth
        copies = fetch(index)
        if kept:
            gates = gate.at[:, part]
        else:
            copies[1].wait()
            gates = buffers[1].at[slot]
        ups = buffers[0].at[slot]
        gate_pre = dot(rows_in[...], gates[...], NN)[:slots]
        copies[0].wait()
        up_pre = dot(rows_in[...], ups[...], NN)[:slots]
        sigmoid = jax.nn.sigmoid(gate_pre)
        grad = act_grad[:, part]
        gate_grad = (grad * up_pre * sigmoid * (1.0 + gate_pre * (1.0 - sigmoid))).astype(BF16)
        up_grad = (grad * gate_pre * sigmoid).astype(BF16)
        for start in range(0, width, chunk):
            rows = pl.ds(start, chunk)
            value = dot(gates[rows, :], gate_grad, NT) + dot(ups[rows, :], up_grad, NT)
            if index > 0:
                value = value + total[rows, :]
            if index < count - 1:
                total[rows, :] = value
            else:
                value = value.T.astype(BF16)
                for piece in range(pieces):
                    outs[piece][:, rows] = value[piece * size : (piece + 1) * size]
        if index + depth < count:
            for copy in reversed(fetch(index + depth)):
                copy.start()


def sum_body(*refs):
    kept, sent = refs[-2:]
    value = refs[0][...].astype(F32)
    for part in refs[1:-2]:
        value = value + part[...].astype(F32)
    kept[...] = value[:CAP]
    sent[...] = value[CAP:]


def sum_all_body(parts, first, second):
    group = parts.shape[0] // EF
    for expert, total in enumerate((first, second)):
        value = parts[expert * group].astype(F32)
        for member in range(1, group):
            value = value + parts[expert * group + member].astype(F32)
        total[...] = value


def place_body(own, base, picks, kept, received, out):
    first = own[0]
    table = jnp.concatenate([slot_table(picks[...], first), slot_table(picks[...], 1 - first)], axis=0)
    total = jnp.concatenate([kept[...], received[...]], axis=0)
    branch = lax.dot_general(table, total, TN, precision=lax.Precision.HIGHEST, preferred_element_type=F32)
    out[...] = (base[...].astype(F32) + branch).astype(BF16)


def hold_body(source, target, sem):
    copy = pltpu.make_async_copy(source, target, sem)
    copy.start()
    copy.wait()


def hold(value):
    return call(
        hold_body,
        pltpu.VMEM(value.shape, value.dtype),
        (value,),
        [HBM],
        "hold",
        1 * MIB,
        scratch_shapes=[pltpu.SemaphoreType.DMA],
    )


def resident(value):
    return pltpu.with_memory_space_constraint(value, pltpu.VMEM)


def call(body, out_shape, args, in_specs, name, limit, **kwargs):
    single = not isinstance(out_shape, (list, tuple))
    args = [
        pltpu.with_memory_space_constraint(arg, pltpu.HBM) if spec is HBM else arg
        for arg, spec in zip(args, in_specs)
    ]
    specs = VMEM if single else [VMEM] * len(out_shape)
    return pl.pallas_call(
        body,
        out_shape=out_shape,
        in_specs=in_specs,
        out_specs=kwargs.pop("out_specs", specs),
        name=name,
        compiler_params=pltpu.CompilerParams(vmem_limit_bytes=limit),
        **kwargs,
    )(*args)


def send(value, target, first=1):
    sizes = [lax.axis_size(axis) for axis in AXES]
    pairs = []
    for pipe in range(first, sizes[0]):
        for expert in range(sizes[1]):
            for data in range(sizes[2]):
                where = target(pipe, expert, data)
                pairs.append(tuple((p * sizes[1] + e) * sizes[2] + d for p, e, d in ((pipe, expert, data), where)))
    return lax.ppermute(value, AXES, pairs)


def to_previous(value):
    return send(value, lambda p, e, d: (p - 1, e, d))


def exchange(value):
    return lax.all_to_all(value, ("expert", "dp"), split_axis=0, concat_axis=0, tiled=True)


def shards(tokens, grad_out, routes, route_weights, gate_weight, up_weight, down_weight):
    members = lax.axis_size("expert") * lax.axis_size("dp")
    lines = lax.axis_size("dp")
    paired = lax.axis_size("expert") == EF and lines & (lines - 1) == 0
    inputs, upstream = tokens[0], grad_out[0]
    picks, pick_weights = routes[0].T, route_weights[0].T
    count, width = inputs.shape
    gate, up, down = gate_weight[0], up_weight[0], down_weight[0]
    hidden = gate.shape[1]
    slots = members * CAP
    shape = jax.ShapeDtypeStruct
    own = lax.axis_index("expert").astype(jnp.int32).reshape(1) if paired else jnp.zeros((1,), jnp.int32)
    sources = (picks, pick_weights, inputs, upstream)
    staging = [pltpu.VMEM(source.shape, source.dtype) for source in sources] + [pltpu.SemaphoreType.DMA((4,))]

    if paired:
        eight = shape((CAP, width), BF16)
        kept_in, kept_grad, sent = call(
            route_body,
            [eight, eight, shape((2, CAP, width), BF16)],
            (own, *sources),
            [SMEM] + [HBM] * 4,
            "route",
            16 * MIB,
            scratch_shapes=staging,
        )
        sent, picks, upstream = lax.optimization_barrier((sent, picks, upstream))
        received = send(sent, lambda p, e, d: (p, 1 - e, d))
        next_upstream = to_previous(upstream)
        next_picks = to_previous(picks)
        sixteen = shape((EF * CAP, width), BF16)
        near_in, near_grad = call(
            join_body, [sixteen, sixteen], (kept_in, kept_grad, received), [VMEM] * 3, "join", 8 * MIB
        )
        order = [step for step in reversed(range(1, lines))]
        far_grad = [send(near_grad, lambda p, e, d, step=step: (p, e, d ^ step)) for step in order]
        far_in = [send(near_in, lambda p, e, d, step=step: (p, e, d ^ step)) for step in order]
        grad_pieces = [near_grad] + far_grad
        in_pieces = [near_in] + far_in
        near_grad, gate = lax.optimization_barrier((near_grad, gate))
        gate = hold(gate)
        grad_pieces, next_picks, gate = lax.optimization_barrier((grad_pieces, next_picks, gate))
    else:
        bound = shape((members, CAP, width), BF16)
        sent_in, sent_grad = call(
            route_all_body,
            [bound, bound],
            sources,
            [HBM] * 4,
            "route",
            32 * MIB,
            scratch_shapes=staging,
        )
        grad_pieces = [exchange(sent_grad).reshape(slots, width)]
        in_pieces = [exchange(sent_in).reshape(slots, width)]
        next_upstream = to_previous(upstream)
        next_picks = to_previous(picks)

    pieces = len(in_pieces)
    block = min(hidden, 512)
    depth = 3
    act_grad = call(
        functools.partial(act_body, pieces=pieces, block=block),
        shape((slots, hidden), F32),
        (*grad_pieces, down),
        [VMEM] * pieces + [HBM],
        "act",
        14 * MIB,
        scratch_shapes=[
            pltpu.VMEM((slots, width), BF16),
            pltpu.VMEM((depth, block, width), BF16),
            pltpu.SemaphoreType.DMA((depth,)),
        ],
    )
    depth = 3
    partial = call(
        functools.partial(back_body, pieces=pieces, block=block, chunk=512, kept=paired),
        [shape((slots // pieces, width), BF16)] * pieces,
        (*in_pieces, act_grad, resident(gate) if paired else gate, up),
        [VMEM] * (pieces + 1) + [VMEM if paired else HBM, HBM],
        "back",
        (20 if paired else 40) * MIB,
        scratch_shapes=[
            pltpu.VMEM((max(128, slots), width), BF16),
            pltpu.VMEM((width, slots), F32),
            *[pltpu.VMEM((depth, width, block), BF16)] * (1 if paired else 2),
            pltpu.SemaphoreType.DMA((2, depth)),
        ],
    )
    total = shape((CAP, width), F32)
    if paired:
        steps = order + [0]
        given = partial[1:] + partial[:1]
        parts = [send(part, lambda p, e, d, step=step: (p - 1, e, d ^ step)) for part, step in zip(given, steps)]
        kept, sent = call(sum_body, [total, total], parts, [VMEM] * pieces, "sum", 16 * MIB)
        received = send(sent, lambda p, e, d: (p, 1 - e, d), first=0)
    else:
        returned = exchange(partial[0].reshape(members, CAP, width))
        kept, received = map(
            to_previous, call(sum_all_body, [total, total], (returned,), [VMEM], "sum", 16 * MIB)
        )
    columns = 768
    out = call(
        place_body,
        shape((count, width), BF16),
        (own, next_upstream, next_picks, kept, received),
        [
            SMEM,
            pl.BlockSpec((count, columns), lambda i: (0, i)),
            pl.BlockSpec(picks.shape, lambda i: (0, 0)),
            pl.BlockSpec((CAP, columns), lambda i: (0, i)),
            pl.BlockSpec((CAP, columns), lambda i: (0, i)),
        ],
        "place",
        16 * MIB,
        grid=(width // columns,),
        out_specs=pl.BlockSpec((count, columns), lambda i: (0, i)),
    )
    return out[None]


def solution(mesh):
    row = P("pipe", ("expert", "dp"), None)
    column = P("pipe", None, ("expert", "dp"))
    return jax.shard_map(
        shards,
        mesh=mesh,
        in_specs=(row, row, row, row, column, column, row),
        out_specs=row,
        check_vma=False,
    )
```

```python
import functools

import jax
import jax.numpy as jnp
from jax import lax
from jax.experimental import pallas as pl
from jax.experimental.pallas import tpu as pltpu
from jax.sharding import PartitionSpec as P

EF = 2
CAP = 8
MIB = 1 << 20
F32 = jnp.float32
BF16 = jnp.bfloat16
NN = (((1,), (0,)), ((), ()))
NT = (((1,), (1,)), ((), ()))
TN = (((0,), (0,)), ((), ()))
VMEM = pl.BlockSpec(memory_space=pltpu.VMEM)
SMEM = pl.BlockSpec(memory_space=pltpu.SMEM)
HBM = pl.BlockSpec(memory_space=pltpu.HBM)
AXES = ("pipe", "expert", "dp")


def dot(a, b, dims):
    return lax.dot_general(a, b, dims, preferred_element_type=F32)


def slot_table(picks, expert):
    count = picks.shape[1]
    chosen = (picks[0:1, :] == expert) | (picks[1:2, :] == expert)
    rows = lax.broadcasted_iota(jnp.int32, (count, count), 0)
    columns = lax.broadcasted_iota(jnp.int32, (count, count), 1)
    before = jnp.where(rows < columns, 1.0, 0.0).astype(BF16)
    flags = jnp.broadcast_to(jnp.where(chosen, 1.0, 0.0), (CAP, count))
    place = dot(flags.astype(BF16), before, NN)
    slots = lax.broadcasted_iota(jnp.int32, (CAP, count), 0).astype(F32)
    return jnp.where(place == slots, flags, 0.0)


def pick_weight(picks, pick_weights, expert):
    first = jnp.where(picks[0:1, :] == expert, pick_weights[0:1, :], 0.0)
    return first + jnp.where(picks[1:2, :] == expert, pick_weights[1:2, :], 0.0)


def select(experts, picks, pick_weights, tokens, upstream):
    tables = [slot_table(picks, expert) for expert in experts]
    weights = [
        jnp.sum(table * pick_weight(picks, pick_weights, expert), axis=1, keepdims=True)
        for table, expert in zip(tables, experts)
    ]
    table = jnp.concatenate(tables, axis=0).astype(BF16)
    sent_in = dot(table, tokens, NN).astype(BF16)
    sent_grad = (jnp.concatenate(weights, axis=0) * dot(table, upstream, NN)).astype(BF16)
    return sent_in, sent_grad, table


def load(sources, targets, sems):
    copies = [
        pltpu.make_async_copy(source, target, sems.at[index])
        for index, (source, target) in enumerate(zip(sources, targets))
    ]
    for copy in copies:
        copy.start()
    for copy in copies:
        copy.wait()
    return [target[...] for target in targets]


def fill(ahead, upstream, table):
    count = upstream.shape[0]
    ahead[:count, :] = upstream
    ahead[count:, :] = jnp.zeros((EF * CAP, ahead.shape[1]), BF16)
    ahead[count:, :count] = table


def route_body(own, picks, pick_weights, tokens, grad_out, kept_in, kept_grad, sent, ahead, *scratch):
    loaded = load((picks, pick_weights, tokens, grad_out), scratch[:-1], scratch[-1])
    first = own[0]
    rows_in, rows_grad, table = select((first, 1 - first), *loaded)
    kept_in[...] = rows_in[:CAP]
    kept_grad[...] = rows_grad[:CAP]
    sent[0] = rows_grad[CAP:]
    sent[1] = rows_in[CAP:]
    fill(ahead, loaded[3], table)


def route_all_body(picks, pick_weights, tokens, grad_out, rows_in, rows_grad, ahead, *scratch):
    loaded = load((picks, pick_weights, tokens, grad_out), scratch[:-1], scratch[-1])
    sent_in, sent_grad, table = select(range(EF), *loaded)
    fill(ahead, loaded[3], table)
    group = rows_in.shape[0] // EF
    for expert in range(EF):
        for member in range(group):
            rows_in[expert * group + member] = sent_in[expert * CAP : (expert + 1) * CAP]
            rows_grad[expert * group + member] = sent_grad[expert * CAP : (expert + 1) * CAP]


def join_body(kept_in, kept_grad, received, rows_in, rows_grad, both):
    rows_in[...] = jnp.concatenate([kept_in[...], received[1]], axis=0)
    rows_grad[...] = jnp.concatenate([kept_grad[...], received[0]], axis=0)
    both[0] = rows_grad[...]
    both[1] = rows_in[...]


def act_body(*refs, pieces, block):
    down, act_grad, rows, buffers, sems = refs[pieces:]
    hidden = down.shape[0]
    count = hidden // block
    depth = buffers.shape[0]

    def fetch(index):
        slot = index % depth
        return pltpu.make_async_copy(down.at[pl.ds(index * block, block), :], buffers.at[slot], sems.at[slot])

    for index in range(min(depth, count)):
        fetch(index).start()
    gather(refs[:pieces], rows, 0)
    for index in range(count):
        fetch(index).wait()
        act_grad[:, pl.ds(index * block, block)] = dot(rows[...], buffers[index % depth], NT)
        if index + depth < count:
            fetch(index + depth).start()


def gather(pieces, rows, which):
    start = 0
    for piece in pieces:
        if len(piece.shape) > 2:
            piece = piece.at[which]
        size = piece.shape[0]
        rows[pl.ds(start, size), :] = piece[...]
        start += size
    if start < rows.shape[0]:
        rows[pl.ds(start, rows.shape[0] - start), :] = jnp.zeros((rows.shape[0] - start, rows.shape[1]), BF16)


def back_body(*refs, pieces, block, chunk):
    act_grad, gate, up = refs[pieces : pieces + 3]
    outs = refs[pieces + 3 : 2 * pieces + 3]
    rows_in, total, *buffers, sems = refs[2 * pieces + 3 :]
    slots = act_grad.shape[0]
    size = slots // pieces
    width, hidden = gate.shape
    count = hidden // block
    depth = buffers[0].shape[0]

    def fetch(index):
        slot = index % depth
        part = pl.ds(index * block, block)
        return [
            pltpu.make_async_copy(source.at[:, part], buffer.at[slot], sems.at[order, slot])
            for order, (source, buffer) in enumerate(zip((up, gate), buffers))
        ]

    for index in range(min(depth, count)):
        for copy in reversed(fetch(index)):
            copy.start()
    gather(refs[:pieces], rows_in, 1)
    for index in range(count):
        part = pl.ds(index * block, block)
        slot = index % depth
        copies = fetch(index)
        copies[1].wait()
        gates = buffers[1].at[slot]
        ups = buffers[0].at[slot]
        gate_pre = dot(rows_in[...], gates[...], NN)[:slots]
        copies[0].wait()
        up_pre = dot(rows_in[...], ups[...], NN)[:slots]
        sigmoid = jax.nn.sigmoid(gate_pre)
        grad = act_grad[:, part]
        gate_grad = (grad * up_pre * sigmoid * (1.0 + gate_pre * (1.0 - sigmoid))).astype(BF16)
        up_grad = (grad * gate_pre * sigmoid).astype(BF16)
        for start in range(0, width, chunk):
            rows = pl.ds(start, chunk)
            value = dot(gates[rows, :], gate_grad, NT) + dot(ups[rows, :], up_grad, NT)
            if index > 0:
                value = value + total[rows, :]
            if index < count - 1:
                total[rows, :] = value
            else:
                value = value.T.astype(BF16)
                for piece in range(pieces):
                    outs[piece][:, rows] = value[piece * size : (piece + 1) * size]
        if index + depth < count:
            for copy in reversed(fetch(index + depth)):
                copy.start()


def sum_body(*refs):
    kept, sent = refs[-2:]
    value = refs[0][...].astype(F32)
    for part in refs[1:-2]:
        value = value + part[...].astype(F32)
    kept[...] = value[:CAP]
    sent[...] = value[CAP:]


def sum_all_body(parts, first, second):
    group = parts.shape[0] // EF
    for expert, total in enumerate((first, second)):
        value = parts[expert * group].astype(F32)
        for member in range(1, group):
            value = value + parts[expert * group + member].astype(F32)
        total[...] = value


def place_body(ahead, kept, received, out, done, sems):
    count, width = out.shape
    table = ahead[count:, :count].astype(F32)
    chunk = width // sems.shape[0]
    copies = []
    for index in range(sems.shape[0]):
        part = pl.ds(index * chunk, chunk)
        total = jnp.concatenate([kept[:, part], received[:, part]], axis=0)
        branch = lax.dot_general(table, total, TN, precision=lax.Precision.HIGHEST, preferred_element_type=F32)
        done[:, part] = (ahead[:count, part].astype(F32) + branch).astype(BF16)
        copies.append(pltpu.make_async_copy(done.at[:, part], out.at[:, part], sems.at[index]))
        copies[-1].start()
    for copy in copies:
        copy.wait()


def call(body, out_shape, args, in_specs, name, limit, **kwargs):
    single = not isinstance(out_shape, (list, tuple))
    args = [
        pltpu.with_memory_space_constraint(arg, pltpu.HBM) if spec is HBM else arg
        for arg, spec in zip(args, in_specs)
    ]
    specs = VMEM if single else [VMEM] * len(out_shape)
    return pl.pallas_call(
        body,
        out_shape=out_shape,
        in_specs=in_specs,
        out_specs=kwargs.pop("out_specs", specs),
        name=name,
        compiler_params=pltpu.CompilerParams(vmem_limit_bytes=limit),
        **kwargs,
    )(*args)


def send(value, target, first=1):
    sizes = [lax.axis_size(axis) for axis in AXES]
    pairs = []
    for pipe in range(first, sizes[0]):
        for expert in range(sizes[1]):
            for data in range(sizes[2]):
                where = target(pipe, expert, data)
                pairs.append(tuple((p * sizes[1] + e) * sizes[2] + d for p, e, d in ((pipe, expert, data), where)))
    return lax.ppermute(value, AXES, pairs)


def to_previous(value):
    return send(value, lambda p, e, d: (p - 1, e, d))


def exchange(value):
    return lax.all_to_all(value, ("expert", "dp"), split_axis=0, concat_axis=0, tiled=True)


def shards(tokens, grad_out, routes, route_weights, gate_weight, up_weight, down_weight):
    members = lax.axis_size("expert") * lax.axis_size("dp")
    lines = lax.axis_size("dp")
    paired = lax.axis_size("expert") == EF and lines & (lines - 1) == 0
    inputs, upstream = tokens[0], grad_out[0]
    picks, pick_weights = routes[0].T, route_weights[0].T
    count, width = inputs.shape
    gate, up, down = gate_weight[0], up_weight[0], down_weight[0]
    hidden = gate.shape[1]
    slots = members * CAP
    shape = jax.ShapeDtypeStruct
    own = lax.axis_index("expert").astype(jnp.int32).reshape(1) if paired else jnp.zeros((1,), jnp.int32)
    sources = (picks, pick_weights, inputs, upstream)
    staging = [pltpu.VMEM(source.shape, source.dtype) for source in sources] + [pltpu.SemaphoreType.DMA((4,))]

    ahead_shape = shape((count + EF * CAP, width), BF16)
    if paired:
        eight = shape((CAP, width), BF16)
        kept_in, kept_grad, sent, ahead = call(
            route_body,
            [eight, eight, shape((2, CAP, width), BF16), ahead_shape],
            (own, *sources),
            [SMEM] + [HBM] * 4,
            "route",
            16 * MIB,
            scratch_shapes=staging,
        )
        received = send(sent, lambda p, e, d: (p, 1 - e, d))
        ahead, received = lax.optimization_barrier((ahead, received))
        sixteen = shape((EF * CAP, width), BF16)
        near_in, near_grad, near_both = call(
            join_body,
            [sixteen, sixteen, shape((2, EF * CAP, width), BF16)],
            (kept_in, kept_grad, received),
            [VMEM] * 3,
            "join",
            8 * MIB,
        )
        order = [step for step in reversed(range(2, lines))]
        far_grad = [send(near_grad, lambda p, e, d, step=step: (p, e, d ^ step)) for step in order]
        both = send(near_both, lambda p, e, d: (p, e, d ^ 1))
        far_in = [send(near_in, lambda p, e, d, step=step: (p, e, d ^ step)) for step in order]
        ahead = to_previous(ahead)
        order = order + [1, 0]
        grad_pieces = far_grad + [both, near_grad]
        in_pieces = far_in + [both, near_in]
        grad_pieces, ahead = lax.optimization_barrier((grad_pieces, ahead))
    else:
        bound = shape((members, CAP, width), BF16)
        sent_in, sent_grad, ahead = call(
            route_all_body,
            [bound, bound, ahead_shape],
            sources,
            [HBM] * 4,
            "route",
            32 * MIB,
            scratch_shapes=staging,
        )
        grad_pieces = [exchange(sent_grad).reshape(slots, width)]
        in_pieces = [exchange(sent_in).reshape(slots, width)]
        ahead = to_previous(ahead)

    pieces = len(in_pieces)
    block = min(hidden, 512)
    depth = 3
    act_grad = call(
        functools.partial(act_body, pieces=pieces, block=block),
        shape((slots, hidden), F32),
        (*grad_pieces, down),
        [VMEM] * pieces + [HBM],
        "act",
        14 * MIB,
        scratch_shapes=[
            pltpu.VMEM((slots, width), BF16),
            pltpu.VMEM((depth, block, width), BF16),
            pltpu.SemaphoreType.DMA((depth,)),
        ],
    )
    depth = 3
    partial = call(
        functools.partial(back_body, pieces=pieces, block=block, chunk=512),
        [shape((slots // pieces, width), BF16)] * pieces,
        (*in_pieces, act_grad, gate, up),
        [VMEM] * (pieces + 1) + [HBM, HBM],
        "back",
        40 * MIB,
        scratch_shapes=[
            pltpu.VMEM((max(128, slots), width), BF16),
            pltpu.VMEM((width, slots), F32),
            pltpu.VMEM((depth, width, block), BF16),
            pltpu.VMEM((depth, width, block), BF16),
            pltpu.SemaphoreType.DMA((2, depth)),
        ],
    )
    total = shape((CAP, width), F32)
    if paired:
        parts = [send(part, lambda p, e, d, step=step: (p - 1, e, d ^ step)) for part, step in zip(partial, order)]
        kept, sent = call(sum_body, [total, total], parts, [VMEM] * pieces, "sum", 16 * MIB)
        received = send(sent, lambda p, e, d: (p, 1 - e, d), first=0)
    else:
        returned = exchange(partial[0].reshape(members, CAP, width))
        kept, received = map(
            to_previous, call(sum_all_body, [total, total], (returned,), [VMEM], "sum", 16 * MIB)
        )
    out = call(
        place_body,
        shape((count, width), BF16),
        (ahead, kept, received),
        [VMEM] * 3,
        "place",
        8 * MIB,
        out_specs=HBM,
        scratch_shapes=[pltpu.VMEM((count, width), BF16), pltpu.SemaphoreType.DMA((4,))],
    )
    return out[None]


def solution(mesh):
    row = P("pipe", ("expert", "dp"), None)
    column = P("pipe", None, ("expert", "dp"))
    return jax.shard_map(
        shards,
        mesh=mesh,
        in_specs=(row, row, row, row, column, column, row),
        out_specs=row,
        check_vma=False,
    )
```

```python
import functools

import jax
import jax.numpy as jnp
from jax import lax
from jax.experimental import pallas as pl
from jax.experimental.pallas import tpu as pltpu
from jax.sharding import PartitionSpec as P

EF = 2
CAP = 8
MIB = 1 << 20
F32 = jnp.float32
BF16 = jnp.bfloat16
NN = (((1,), (0,)), ((), ()))
NT = (((1,), (1,)), ((), ()))
TN = (((0,), (0,)), ((), ()))
VMEM = pl.BlockSpec(memory_space=pltpu.VMEM)
SMEM = pl.BlockSpec(memory_space=pltpu.SMEM)
HBM = pl.BlockSpec(memory_space=pltpu.HBM)
AXES = ("pipe", "expert", "dp")


def dot(a, b, dims):
    return lax.dot_general(a, b, dims, preferred_element_type=F32)


def slot_table(picks, expert):
    count = picks.shape[1]
    chosen = (picks[0:1, :] == expert) | (picks[1:2, :] == expert)
    rows = lax.broadcasted_iota(jnp.int32, (count, count), 0)
    columns = lax.broadcasted_iota(jnp.int32, (count, count), 1)
    before = jnp.where(rows < columns, 1.0, 0.0).astype(BF16)
    flags = jnp.broadcast_to(jnp.where(chosen, 1.0, 0.0), (CAP, count))
    place = dot(flags.astype(BF16), before, NN)
    slots = lax.broadcasted_iota(jnp.int32, (CAP, count), 0).astype(F32)
    return jnp.where(place == slots, flags, 0.0)


def pick_weight(picks, pick_weights, expert):
    first = jnp.where(picks[0:1, :] == expert, pick_weights[0:1, :], 0.0)
    return first + jnp.where(picks[1:2, :] == expert, pick_weights[1:2, :], 0.0)


def select(experts, picks, pick_weights, tokens, upstream):
    tables = [slot_table(picks, expert) for expert in experts]
    weights = [
        jnp.sum(table * pick_weight(picks, pick_weights, expert), axis=1, keepdims=True)
        for table, expert in zip(tables, experts)
    ]
    table = jnp.concatenate(tables, axis=0).astype(BF16)
    sent_in = dot(table, tokens, NN).astype(BF16)
    sent_grad = (jnp.concatenate(weights, axis=0) * dot(table, upstream, NN)).astype(BF16)
    return sent_in, sent_grad, table


def load(sources, targets, sems):
    copies = [
        pltpu.make_async_copy(source, target, sems.at[index])
        for index, (source, target) in enumerate(zip(sources, targets))
    ]
    for copy in copies:
        copy.start()
    for copy in copies:
        copy.wait()
    return [target[...] for target in targets]


def fill(ahead, upstream, table):
    count = upstream.shape[0]
    ahead[:count, :] = upstream
    ahead[count:, :] = jnp.zeros((EF * CAP, ahead.shape[1]), BF16)
    ahead[count:, :count] = table


def route_body(own, picks, pick_weights, tokens, grad_out, kept_in, kept_grad, sent, ahead, *scratch):
    loaded = load((picks, pick_weights, tokens, grad_out), scratch[:-1], scratch[-1])
    first = own[0]
    rows_in, rows_grad, table = select((first, 1 - first), *loaded)
    kept_in[...] = rows_in[:CAP]
    kept_grad[...] = rows_grad[:CAP]
    sent[0] = rows_grad[CAP:]
    sent[1] = rows_in[CAP:]
    fill(ahead, loaded[3], table)


def route_all_body(picks, pick_weights, tokens, grad_out, rows_in, rows_grad, ahead, *scratch):
    loaded = load((picks, pick_weights, tokens, grad_out), scratch[:-1], scratch[-1])
    sent_in, sent_grad, table = select(range(EF), *loaded)
    fill(ahead, loaded[3], table)
    group = rows_in.shape[0] // EF
    for expert in range(EF):
        for member in range(group):
            rows_in[expert * group + member] = sent_in[expert * CAP : (expert + 1) * CAP]
            rows_grad[expert * group + member] = sent_grad[expert * CAP : (expert + 1) * CAP]


def join_body(kept_in, kept_grad, received, rows_in, rows_grad, both):
    rows_in[...] = jnp.concatenate([kept_in[...], received[1]], axis=0)
    rows_grad[...] = jnp.concatenate([kept_grad[...], received[0]], axis=0)
    both[0] = rows_grad[...]
    both[1] = rows_in[...]


def act_body(*refs, pieces, block):
    down, gate, up, act_grad, gate_first, up_first, rows, buffers, sems, first_sems = refs[pieces:]
    hidden = down.shape[0]
    early = [
        pltpu.make_async_copy(source.at[:, pl.ds(0, block)], target, first_sems.at[order])
        for order, (source, target) in enumerate(((gate, gate_first), (up, up_first)))
    ]
    count = hidden // block
    depth = buffers.shape[0]

    def fetch(index):
        slot = index % depth
        return pltpu.make_async_copy(down.at[pl.ds(index * block, block), :], buffers.at[slot], sems.at[slot])

    for index in range(min(depth, count)):
        fetch(index).start()
    gather(refs[:pieces], rows, 0)
    for index in range(count):
        fetch(index).wait()
        act_grad[:, pl.ds(index * block, block)] = dot(rows[...], buffers[index % depth], NT)
        if index + depth < count:
            fetch(index + depth).start()
        elif index + depth == max(count, depth):
            for copy in early:
                copy.start()
    for copy in early:
        copy.wait()


def gather(pieces, rows, which):
    start = 0
    for piece in pieces:
        if len(piece.shape) > 2:
            piece = piece.at[which]
        size = piece.shape[0]
        rows[pl.ds(start, size), :] = piece[...]
        start += size
    if start < rows.shape[0]:
        rows[pl.ds(start, rows.shape[0] - start), :] = jnp.zeros((rows.shape[0] - start, rows.shape[1]), BF16)


def back_body(*refs, pieces, block, chunk):
    act_grad, gate, up, gate_first, up_first = refs[pieces : pieces + 5]
    outs = refs[pieces + 5 : 2 * pieces + 5]
    rows_in, total, *buffers, sems = refs[2 * pieces + 5 :]
    slots = act_grad.shape[0]
    size = slots // pieces
    width, hidden = gate.shape
    count = hidden // block
    depth = buffers[0].shape[0]

    def fetch(index):
        slot = index % depth
        part = pl.ds(index * block, block)
        return [
            pltpu.make_async_copy(source.at[:, part], buffer.at[slot], sems.at[order, slot])
            for order, (source, buffer) in enumerate(zip((up, gate), buffers))
        ]

    for index in range(1, min(depth + 1, count)):
        for copy in reversed(fetch(index)):
            copy.start()
    gather(refs[:pieces], rows_in, 1)
    for index in range(count):
        part = pl.ds(index * block, block)
        slot = index % depth
        copies = fetch(index) if index else None
        gates, ups = (buffers[1].at[slot], buffers[0].at[slot]) if index else (gate_first, up_first)
        if index:
            copies[1].wait()
        gate_pre = dot(rows_in[...], gates[...], NN)[:slots]
        if index:
            copies[0].wait()
        up_pre = dot(rows_in[...], ups[...], NN)[:slots]
        sigmoid = jax.nn.sigmoid(gate_pre)
        grad = act_grad[:, part]
        gate_grad = (grad * up_pre * sigmoid * (1.0 + gate_pre * (1.0 - sigmoid))).astype(BF16)
        up_grad = (grad * gate_pre * sigmoid).astype(BF16)
        for start in range(0, width, chunk):
            rows = pl.ds(start, chunk)
            value = dot(gates[rows, :], gate_grad, NT) + dot(ups[rows, :], up_grad, NT)
            if index > 0:
                value = value + total[rows, :]
            if index < count - 1:
                total[rows, :] = value
            else:
                value = value.T.astype(BF16)
                for piece in range(pieces):
                    outs[piece][:, rows] = value[piece * size : (piece + 1) * size]
        if index and index + depth < count:
            for copy in reversed(fetch(index + depth)):
                copy.start()


def sum_body(*refs):
    kept, sent = refs[-2:]
    value = refs[0][...].astype(F32)
    for part in refs[1:-2]:
        value = value + part[...].astype(F32)
    kept[...] = value[:CAP]
    sent[...] = value[CAP:]


def sum_all_body(parts, first, second):
    group = parts.shape[0] // EF
    for expert, total in enumerate((first, second)):
        value = parts[expert * group].astype(F32)
        for member in range(1, group):
            value = value + parts[expert * group + member].astype(F32)
        total[...] = value


def place_body(ahead, kept, received, out, done, sems):
    count, width = out.shape
    table = ahead[count:, :count].astype(F32)
    chunk = width // sems.shape[0]
    copies = []
    for index in range(sems.shape[0]):
        part = pl.ds(index * chunk, chunk)
        total = jnp.concatenate([kept[:, part], received[:, part]], axis=0)
        branch = lax.dot_general(table, total, TN, precision=lax.Precision.HIGHEST, preferred_element_type=F32)
        done[:, part] = (ahead[:count, part].astype(F32) + branch).astype(BF16)
        copies.append(pltpu.make_async_copy(done.at[:, part], out.at[:, part], sems.at[index]))
        copies[-1].start()
    for copy in copies:
        copy.wait()


def resident(value):
    return pltpu.with_memory_space_constraint(value, pltpu.VMEM)


def call(body, out_shape, args, in_specs, name, limit, **kwargs):
    single = not isinstance(out_shape, (list, tuple))
    args = [
        pltpu.with_memory_space_constraint(arg, pltpu.HBM) if spec is HBM else arg
        for arg, spec in zip(args, in_specs)
    ]
    specs = VMEM if single else [VMEM] * len(out_shape)
    return pl.pallas_call(
        body,
        out_shape=out_shape,
        in_specs=in_specs,
        out_specs=kwargs.pop("out_specs", specs),
        name=name,
        compiler_params=pltpu.CompilerParams(vmem_limit_bytes=limit),
        **kwargs,
    )(*args)


def send(value, target, first=1):
    sizes = [lax.axis_size(axis) for axis in AXES]
    pairs = []
    for pipe in range(first, sizes[0]):
        for expert in range(sizes[1]):
            for data in range(sizes[2]):
                where = target(pipe, expert, data)
                pairs.append(tuple((p * sizes[1] + e) * sizes[2] + d for p, e, d in ((pipe, expert, data), where)))
    return lax.ppermute(value, AXES, pairs)


def to_previous(value):
    return send(value, lambda p, e, d: (p - 1, e, d))


def exchange(value):
    return lax.all_to_all(value, ("expert", "dp"), split_axis=0, concat_axis=0, tiled=True)


def shards(tokens, grad_out, routes, route_weights, gate_weight, up_weight, down_weight):
    members = lax.axis_size("expert") * lax.axis_size("dp")
    lines = lax.axis_size("dp")
    paired = lax.axis_size("expert") == EF and lines & (lines - 1) == 0
    inputs, upstream = tokens[0], grad_out[0]
    picks, pick_weights = routes[0].T, route_weights[0].T
    count, width = inputs.shape
    gate, up, down = gate_weight[0], up_weight[0], down_weight[0]
    hidden = gate.shape[1]
    slots = members * CAP
    shape = jax.ShapeDtypeStruct
    own = lax.axis_index("expert").astype(jnp.int32).reshape(1) if paired else jnp.zeros((1,), jnp.int32)
    sources = (picks, pick_weights, inputs, upstream)
    staging = [pltpu.VMEM(source.shape, source.dtype) for source in sources] + [pltpu.SemaphoreType.DMA((4,))]

    ahead_shape = shape((count + EF * CAP, width), BF16)
    if paired:
        eight = shape((CAP, width), BF16)
        kept_in, kept_grad, sent, ahead = call(
            route_body,
            [eight, eight, shape((2, CAP, width), BF16), ahead_shape],
            (own, *sources),
            [SMEM] + [HBM] * 4,
            "route",
            16 * MIB,
            scratch_shapes=staging,
        )
        received = send(sent, lambda p, e, d: (p, 1 - e, d))
        ahead, received = lax.optimization_barrier((ahead, received))
        sixteen = shape((EF * CAP, width), BF16)
        near_in, near_grad, near_both = call(
            join_body,
            [sixteen, sixteen, shape((2, EF * CAP, width), BF16)],
            (kept_in, kept_grad, received),
            [VMEM] * 3,
            "join",
            8 * MIB,
        )
        order = [step for step in reversed(range(2, lines))]
        far_grad = [send(near_grad, lambda p, e, d, step=step: (p, e, d ^ step)) for step in order]
        both = send(near_both, lambda p, e, d: (p, e, d ^ 1))
        far_in = [send(near_in, lambda p, e, d, step=step: (p, e, d ^ step)) for step in order]
        ahead = to_previous(ahead)
        order = order + [1, 0]
        grad_pieces = far_grad + [both, near_grad]
        in_pieces = far_in + [both, near_in]
        grad_pieces, ahead = lax.optimization_barrier((grad_pieces, ahead))
    else:
        bound = shape((members, CAP, width), BF16)
        sent_in, sent_grad, ahead = call(
            route_all_body,
            [bound, bound, ahead_shape],
            sources,
            [HBM] * 4,
            "route",
            32 * MIB,
            scratch_shapes=staging,
        )
        grad_pieces = [exchange(sent_grad).reshape(slots, width)]
        in_pieces = [exchange(sent_in).reshape(slots, width)]
        ahead = to_previous(ahead)

    pieces = len(in_pieces)
    block = min(hidden, 512)
    depth = 3
    first_block = pltpu.VMEM((width, block), BF16)
    act_grad, gate_first, up_first = call(
        functools.partial(act_body, pieces=pieces, block=block),
        [shape((slots, hidden), F32), first_block, first_block],
        (*grad_pieces, down, gate, up),
        [VMEM] * pieces + [HBM] * 3,
        "act",
        16 * MIB,
        scratch_shapes=[
            pltpu.VMEM((slots, width), BF16),
            pltpu.VMEM((depth, block, width), BF16),
            pltpu.SemaphoreType.DMA((depth,)),
            pltpu.SemaphoreType.DMA((2,)),
        ],
    )
    depth = 3
    partial = call(
        functools.partial(back_body, pieces=pieces, block=block, chunk=512),
        [shape((slots // pieces, width), BF16)] * pieces,
        (*in_pieces, act_grad, gate, up, resident(gate_first), resident(up_first)),
        [VMEM] * (pieces + 1) + [HBM, HBM, VMEM, VMEM],
        "back",
        40 * MIB,
        scratch_shapes=[
            pltpu.VMEM((max(128, slots), width), BF16),
            pltpu.VMEM((width, slots), F32),
            pltpu.VMEM((depth, width, block), BF16),
            pltpu.VMEM((depth, width, block), BF16),
            pltpu.SemaphoreType.DMA((2, depth)),
        ],
    )
    total = shape((CAP, width), F32)
    if paired:
        parts = [send(part, lambda p, e, d, step=step: (p - 1, e, d ^ step)) for part, step in zip(partial, order)]
        kept, sent = call(sum_body, [total, total], parts, [VMEM] * pieces, "sum", 16 * MIB)
        received = send(sent, lambda p, e, d: (p, 1 - e, d), first=0)
    else:
        returned = exchange(partial[0].reshape(members, CAP, width))
        kept, received = map(
            to_previous, call(sum_all_body, [total, total], (returned,), [VMEM], "sum", 16 * MIB)
        )
    out = call(
        place_body,
        shape((count, width), BF16),
        (ahead, kept, received),
        [VMEM] * 3,
        "place",
        8 * MIB,
        out_specs=HBM,
        scratch_shapes=[pltpu.VMEM((count, width), BF16), pltpu.SemaphoreType.DMA((4,))],
    )
    return out[None]


def solution(mesh):
    row = P("pipe", ("expert", "dp"), None)
    column = P("pipe", None, ("expert", "dp"))
    return jax.shard_map(
        shards,
        mesh=mesh,
        in_specs=(row, row, row, row, column, column, row),
        out_specs=row,
        check_vma=False,
    )
```
